32 devices in a mesh: shard: 8 (over z, y), rep: 4 (over x, core).
Axes of the slice: x: 2, y: 2, z: 4, core: 2. Of those that a mesh axis runs over, the one named last changes fastest.
Arguments:
- queries: bfloat16 [4, 8, 32, 128], P('rep', 'shard'), may hold values from -0.5 to 0.5
- candidates: int32 [4, 8, 64], P('rep', 'shard'), may hold values from 0 to 127, all different within a row; in each aligned block of 8 rows (0 to 7, 8 to 15, ..., all dimensions but the last counted through in order) at most 8 rows name the same one
- codebook: bfloat16 [32768, 128], P(('shard', 'rep')), may hold values from -0.5 to 0.5
- bucket_weights: float32 [4], replicated, may hold values from -0.1 to 0.1
- centroid_ids: int32 [128, 128], P('shard'), may hold values from 0 to 4095
- residual_codes: int32 [128, 128, 128], P('shard'), may hold values from 0 to 3
- passage_lengths: int32 [128], P('shard'), may hold values from 1 to 128, 12288 in all
Outputs:
- best_centroid: float32 [4, 8, 32], P('rep', 'shard')
- scores: float32 [4, 8, 64], P('rep', 'shard')
The draws below stay inside these ranges and needn't reach their ends.
Inputs may be any that keep to these rules, and one draw needn't show every extreme that they name: `candidates`: each query names 64 different passages. Within the 8 queries of one index of rep, no passage is named by more than 8 queries, a bound that some block reaches. `passage_lengths`: some passage has all 128 slots live.
All inputs are finite; a program needn't handle non-finite values. No bound on the sum of `passage_lengths` on one device may be relied on, other than what follows from the above.
Results may differ from the reference program's by a relative error of at most 0.00045.
Values may be sent and summed in bfloat16 or wider, within the bound.
No kernel may reach another device: no remote copies, remote signals or barrier semaphores. Data moves between devices by JAX's collectives and lax.ppermute only.
A program may use at most 64 MiB of HBM per device.

```python
import math
import jax
import jax.numpy as jnp
import numpy as np
from jax import lax

DIM = 128
QT = 32
PT = 128
SHARD_CENT = 4096
NCENT = 32768
BUCKETS = 4
QG = 8
PDEV = 16
NPASS = 128
NCAND = 64
MOST = 8
N_SHARD = 8
N_REP = 4


def place_ends(drawn, stream_key, smallest, largest):
    dims = drawn.shape
    spot = [jax.random.randint(jax.random.fold_in(stream_key, axis), (), 0, dims[axis]) for axis in range(len(dims))]
    drawn = drawn.at[tuple(spot)].set(smallest)
    longest = dims.index(max(dims))
    spot[longest] = (spot[longest] + 1) % dims[longest]
    return drawn.at[tuple(spot)].set(largest)


def level_of(stream_key, shape, shards, low, high):
    loudness = 1.0
    for dim, blocks in shards:
        draws = jax.random.uniform(jax.random.fold_in(jax.random.fold_in(stream_key, 6), dim), (blocks,), jnp.float32, low / len(shards), high / len(shards))
        loudness = loudness * jnp.repeat(jnp.exp(draws), shape[dim] // blocks).reshape((-1,) + (1,) * (len(shape) - 1 - dim))
    return loudness


def profile(number_of, total, most, slope):
    loads = [(1 << 20) // math.isqrt(grade ** slope) + 1 for grade in range(2, number_of + 1)]
    surplus, given = total - most - (number_of - 1), [1] * (number_of - 1)
    while surplus > 0:
        free = [i for i in range(number_of - 1) if given[i] < most]
        mass, budget = sum([loads[i] for i in free]), surplus
        for i in free:
            addition = min(most - given[i], max(1, budget * loads[i] // mass), surplus)
            given[i] = given[i] + addition
            surplus = surplus - addition
    return np.array([most] + given)


def uneven(rng, count, total, reach, slope):
    if count == 2:
        one = jax.random.randint(rng, (), max(1, total - reach), min(reach, total - 1) + 1)
        return jnp.stack([one, total - one])
    sizes = jnp.asarray(profile(count, total, reach, slope), jnp.int32)
    twos = (count - 1) // 2
    giver, receiver = sizes[1:1 + 2 * twos:2], sizes[2:2 + 2 * twos:2]
    margin = jnp.minimum(giver - 1, reach - receiver)
    moved = jax.random.randint(jax.random.fold_in(rng, 1), (twos,), 0, 1 << 20) % (margin + 1)
    sizes = sizes.at[1:1 + 2 * twos:2].set(giver - moved).at[2:2 + 2 * twos:2].set(receiver + moved)
    return sizes[jax.random.permutation(jax.random.fold_in(rng, 2), count)]


def assign_block(key, own, number, rows, amount, top, limit, lean):
    ranking = jax.random.permutation(key, amount)
    crowded, ordinary = load_shares(amount, rows * top, limit, lean, True), load_shares(amount, rows * top, limit, lean, False)
    places = jnp.arange(amount)

    def named(tallies, rotation):
        used = int((tallies > 0).sum())
        fixed = max(1, used // 4)
        passed = fixed + (places - fixed + rotation * (used - fixed)) % max(1, amount - fixed)
        return jnp.zeros((amount,), jnp.int32).at[ranking[jnp.where(places < fixed, places, passed)]].set(jnp.asarray(tallies, jnp.int32))

    tallies = jnp.where(number % 4 == 0, named(crowded, number // 4), named(ordinary, number - number // 4 - 1))
    mixed = jax.random.permutation(jax.random.fold_in(own, 3), amount)
    source_of, sink = mixed[0:amount // 2 * 2:2], mixed[1:amount // 2 * 2:2]
    room = jnp.minimum(tallies[source_of] - 1, limit - tallies[sink]) // 2
    room = jnp.where((source_of == ranking[0]) | (sink == ranking[0]) | (tallies[sink] == 0), 0, jnp.maximum(room, 0))
    passed = jax.random.randint(jax.random.fold_in(own, 4), (amount // 2,), 0, 1 << 20) % (room + 1)
    tallies = tallies.at[source_of].add(-passed).at[sink].add(passed)
    items = jnp.searchsorted(jnp.cumsum(tallies), jnp.arange(rows * top), side="right").astype(jnp.int32)
    table = items.reshape(top, rows).T
    table = table[jax.random.permutation(jax.random.fold_in(own, 1), rows)]
    rotation = jax.random.randint(jax.random.fold_in(own, 2), (rows, 1), 0, top)
    return jnp.take_along_axis(table, (jnp.arange(top)[None, :] + rotation) % top, axis=1)


def load_shares(amount, total, bound, lean, full):
    weights = [(1 << 20) // math.isqrt(standing ** lean) + 1 for standing in range(1, amount + 1)]
    largest = bound if full else min(bound, max(-(-total // amount), total * weights[0] // sum(weights)))
    least = 1 if total - largest >= amount - 1 else 0
    holding, rest = [largest] + [least] * (amount - 1), total - largest - least * (amount - 1)
    while rest > 0:
        movable = [i for i in range(1, amount) if holding[i] < largest] or [i for i in range(1, amount) if holding[i] < bound]
        whole, remaining = sum([weights[i] for i in movable]), rest
        for i in movable:
            extra = min(bound - holding[i], max(1, remaining * weights[i] // whole), rest)
            holding[i] = holding[i] + extra
            rest = rest - extra
    return np.array(holding)


def scatter_about(own_key, shape, spread, most, shards=(), kind=jnp.bfloat16):
    factor_of = level_of(own_key, shape, shards, -0.22, 0.18) if shards else 1.0
    result = jax.random.normal(own_key, shape, jnp.float32) * spread * factor_of
    return jnp.minimum(jnp.maximum(result, -most), most).astype(kind)


def setup_inputs(seed: int = 0) -> dict:
    streams_of = jax.random.split(jax.random.key(seed), 8)
    queries = scatter_about(streams_of[0], (N_REP, QG, QT, DIM), 0.088, 0.5, ((0, 4), (1, 8)))
    candidates_keys = jax.random.split(jax.random.fold_in(streams_of[1], 1), N_REP * QG // QG)
    candidates_turns = jax.random.permutation(jax.random.fold_in(streams_of[1], 3), N_REP * QG // QG)
    candidates = jax.vmap(lambda own, number: assign_block(jax.random.fold_in(streams_of[1], 2), own, number, QG, NPASS, NCAND, MOST, 2))(candidates_keys, candidates_turns).reshape((N_REP, QG, NCAND))
    codebook = scatter_about(streams_of[2], (NCENT, DIM), 0.088, 0.5, ((0, 32),))
    bucket_weights = jnp.clip(jax.random.uniform(streams_of[3], (BUCKETS,), jnp.float32, -0.1, 0.1), -0.1, 0.1)
    centroid_ids = place_ends(jax.random.randint(streams_of[4], (NPASS, PT), 0, SHARD_CENT), jax.random.fold_in(streams_of[4], 1), 0, SHARD_CENT - 1).astype(jnp.int32)
    residual_codes = place_ends(jax.random.randint(streams_of[5], (NPASS, PT, DIM), 0, BUCKETS), jax.random.fold_in(streams_of[5], 1), 0, BUCKETS - 1).astype(jnp.int32)
    passage_lengths = uneven(streams_of[6], NPASS, NPASS * PT * 3 // 4, PT, 1).astype(jnp.int32)
    return dict(queries=queries, candidates=candidates, codebook=codebook, bucket_weights=bucket_weights, centroid_ids=centroid_ids, residual_codes=residual_codes, passage_lengths=passage_lengths)


def reference(queries, candidates, codebook, bucket_weights, centroid_ids, residual_codes, passage_lengths):
    token_rows = queries.reshape(N_REP * QG * QT, DIM)
    books = codebook.reshape(N_SHARD, SHARD_CENT, DIM)

    def fold_step(running, shard_book):
        scored = jnp.dot(token_rows, shard_book.T, preferred_element_type=jnp.float32)
        return jnp.maximum(running, jnp.max(scored, axis=1)), None

    initial = jnp.full((N_REP * QG * QT,), -1e30, dtype=jnp.float32)
    best_flat, unused = lax.scan(fold_step, initial, books)
    best_centroid = best_flat.reshape(N_REP, QG, QT)

    owners = jnp.arange(NPASS, dtype=jnp.int32) // PDEV
    row_ids = (owners[:, None] * SHARD_CENT + centroid_ids).astype(jnp.int32)
    residual = jnp.take(bucket_weights, residual_codes)
    embedded = (jnp.take(codebook, row_ids, axis=0).astype(jnp.float32) + residual).astype(jnp.bfloat16)
    live_mask = jnp.arange(PT, dtype=jnp.int32)[None, :] < passage_lengths[:, None]

    def one_query(pair_args):
        query_tokens, cand_ids = pair_args
        picked = jnp.take(embedded, cand_ids, axis=0).astype(jnp.float32)
        picked_live = jnp.take(live_mask, cand_ids, axis=0)
        similar = jnp.einsum("td,cpd->ctp", query_tokens.astype(jnp.float32), picked)
        similar = jnp.where(picked_live[:, None, :], similar, -1e30)
        return jnp.sum(jnp.max(similar, axis=2), axis=1)

    scores = lax.map(one_query, (queries.reshape(N_REP * QG, QT, DIM), candidates.reshape(N_REP * QG, NCAND)))
    return best_centroid, scores.reshape(N_REP, QG, NCAND)
```

```python
import functools

import jax
import jax.numpy as jnp
from jax import lax
from jax.experimental import pallas as pl
from jax.experimental.pallas import tpu as pltpu
from jax.sharding import PartitionSpec as P

FAR_BELOW = -1e30
LANES = 128
LOW = 256
EXACT = lax.Precision.HIGHEST


def exchange(value, axis, mask):
    count = lax.axis_size(axis)
    return lax.ppermute(value, axis, [(i, i ^ mask) for i in range(count)])


def gather_by_xor(block, axis):
    count = lax.axis_size(axis)
    held = block[None]
    reach = 1
    while reach < count:
        step = 2 if reach == 1 or reach * 2 == count else 4
        parts = [exchange(held, axis, reach * k) for k in range(1, step)]
        held = jnp.concatenate([held] + parts, axis=0)
        reach *= step
    return held


def embed_kernel(rep_ref, weight_ref, ids_ref, codes_ref, *refs):
    *book_refs, out_ref, onehot_ref, high_ref, sum_ref = refs
    passages, slots = ids_ref.shape
    block_rows = book_refs[0].shape[0]
    rows = passages * slots
    ids_by_slot = jnp.transpose(ids_ref[...])
    lane = lax.broadcasted_iota(jnp.int32, (slots, LANES), 1)
    levels = weight_ref.shape[0]
    for p in range(passages):
        here = pl.ds(p * slots, slots)
        ids = jnp.broadcast_to(ids_by_slot[:, p : p + 1], (slots, LANES))
        low = ids & (LOW - 1)
        onehot_ref[here, :] = jnp.concatenate(
            [(low == lane + k * LANES).astype(jnp.float32) for k in range(LOW // LANES)], axis=1
        ).astype(jnp.bfloat16)
        high_ref[here, :] = ids >> (LOW.bit_length() - 1)
        sum_ref[here, :] = jnp.zeros((slots, LANES), jnp.float32)
    chunk = slots
    for k, book_ref in enumerate(book_refs):
        first = (rep_ref[0] ^ k) * (block_rows // LOW)
        for j in range(0, block_rows // LOW, 2):
            pair = jnp.concatenate(
                [book_ref[(j + h) * LOW : (j + h + 1) * LOW, :] for h in range(2)], axis=1
            )
            for c in range(rows // chunk):
                here = pl.ds(c * chunk, chunk)
                found = jnp.dot(onehot_ref[here, :], pair, preferred_element_type=jnp.float32)
                high = high_ref[here, :]
                total = sum_ref[here, :]
                for h in range(2):
                    total = jnp.where(high == first + (j + h), found[:, h * LANES : (h + 1) * LANES], total)
                sum_ref[here, :] = total
    for p in range(passages):
        here = pl.ds(p * slots, slots)
        codes = codes_ref[p]
        residual = jnp.full(codes.shape, weight_ref[levels - 1], jnp.float32)
        for level in range(levels - 2, -1, -1):
            residual = jnp.where(codes == level, weight_ref[level], residual)
        out_ref[here, :] = (sum_ref[here, :] + residual).astype(jnp.bfloat16)


def score_kernel(tokens, shard_ref, length_ref, query_ref, embedded_ref, *refs):
    *book_refs, out_ref = refs
    passages = length_ref.shape[0]
    slots = embedded_ref.shape[0] // passages
    width = query_ref.shape[0]
    count = width // tokens
    queries = query_ref[...]

    def product(rows):
        return lax.dot_general(
            rows, queries, (((1,), (1,)), ((), ())), preferred_element_type=jnp.float32
        )

    best = jnp.full((8, width), FAR_BELOW, jnp.float32)
    chunk = 128
    for book_ref in book_refs:
        for c in range(book_ref.shape[0] // chunk):
            found = product(book_ref[c * chunk : (c + 1) * chunk, :])
            best = jnp.maximum(best, jnp.max(found.reshape(chunk // 8, 8, width), axis=0))
    best = jnp.max(best, axis=0, keepdims=True)
    slot = lax.broadcasted_iota(jnp.int32, (slots, width), 0)
    tops = []
    for p in range(passages):
        found = product(embedded_ref[p * slots : (p + 1) * slots, :])
        found = jnp.where(slot < length_ref[p], found, FAR_BELOW)
        tops.append(jnp.max(found, axis=0, keepdims=True))
    lane_room = out_ref.shape[1]
    table = jnp.concatenate(
        [jnp.zeros((tokens, width), jnp.float32)]
        + tops
        + [jnp.zeros((lane_room - tokens - passages, width), jnp.float32)],
        axis=0,
    )
    mine = (
        lax.broadcasted_iota(jnp.int32, (count, width), 1) // tokens
        == lax.broadcasted_iota(jnp.int32, (count, width), 0)
    ).astype(jnp.float32)
    sums = lax.dot_general(
        mine, table, (((1,), (1,)), ((), ())), preferred_element_type=jnp.float32, precision=EXACT
    )
    start = pl.program_id(0) * count
    for q in range(count):
        row = pl.ds((start + q) ^ shard_ref[0], 1)
        out_ref[row, :] = sums[q : q + 1, :]
        out_ref[row, 0:tokens] = best[:, q * tokens : (q + 1) * tokens]


def finish_kernel(tokens, passages, table_ref, cands_ref, best_ref, scores_ref):
    table = table_ref[...]
    shards, room = table.shape
    best_ref[...] = jnp.max(table, axis=0, keepdims=True)[:, 0:tokens]
    cands = cands_ref[...]
    count = cands.shape[1]
    owner = (lax.broadcasted_iota(jnp.int32, (shards, count), 0) == cands // passages).astype(jnp.float32)
    columns = lax.dot_general(
        table, owner, (((0,), (0,)), ((), ())), preferred_element_type=jnp.float32, precision=EXACT
    )
    wanted = lax.broadcasted_iota(jnp.int32, (room, count), 0) == tokens + cands % passages
    scores_ref[...] = jnp.sum(jnp.where(wanted, columns, 0.0), axis=0, keepdims=True)


def on_device(queries, candidates, codebook, bucket_weights, centroid_ids, residual_codes, passage_lengths):
    tokens, features = queries.shape[2:]
    passages, slots = centroid_ids.shape
    shards, reps = lax.axis_size("shard"), lax.axis_size("rep")
    vmem = pl.BlockSpec(memory_space=pltpu.VMEM)
    smem = pl.BlockSpec(memory_space=pltpu.SMEM)
    shard = lax.axis_index("shard").astype(jnp.int32).reshape(1)
    rep = lax.axis_index("rep").astype(jnp.int32).reshape(1)

    books = {0: codebook}
    bit = reps // 2
    while bit:
        for k in list(books):
            books[k ^ bit] = exchange(books[k], "rep", bit)
        bit //= 2
    books = [books[k] for k in range(reps)]
    group = gather_by_xor(queries[0, 0], "shard").reshape(shards * tokens, features)

    rows = passages * slots
    embedded = pl.pallas_call(
        embed_kernel,
        out_shape=jax.ShapeDtypeStruct((rows, features), jnp.bfloat16),
        in_specs=[smem, smem] + [vmem] * (2 + reps),
        out_specs=vmem,
        scratch_shapes=[
            pltpu.VMEM((rows, LOW), jnp.bfloat16),
            pltpu.VMEM((rows, LANES), jnp.int32),
            pltpu.VMEM((rows, features), jnp.float32),
        ],
        compiler_params=pltpu.CompilerParams(vmem_limit_bytes=24 << 20),
        cost_estimate=pl.CostEstimate(flops=2 * rows * LOW * features * 16, bytes_accessed=2 << 20, transcendentals=0),
    )(rep, bucket_weights, centroid_ids, residual_codes, *books)

    room = -(-(tokens + passages) // LANES) * LANES
    width = 256
    packed = pl.pallas_call(
        functools.partial(score_kernel, tokens),
        out_shape=jax.ShapeDtypeStruct((shards, room), jnp.float32),
        grid=(shards * tokens // width,),
        in_specs=[smem, smem, pl.BlockSpec((width, features), lambda i: (i, 0))] + [vmem] * (1 + reps),
        out_specs=vmem,
        compiler_params=pltpu.CompilerParams(vmem_limit_bytes=24 << 20),
        cost_estimate=pl.CostEstimate(flops=2 * 6144 * 256 * features, bytes_accessed=2 << 20, transcendentals=0),
    )(shard, passage_lengths, group, embedded, *books)

    table = lax.all_to_all(packed, "shard", split_axis=0, concat_axis=0, tiled=True)
    best, scores = pl.pallas_call(
        functools.partial(finish_kernel, tokens, passages),
        out_shape=(
            jax.ShapeDtypeStruct((1, tokens), jnp.float32),
            jax.ShapeDtypeStruct((1, candidates.shape[2]), jnp.float32),
        ),
        in_specs=[vmem, vmem],
        out_specs=(vmem, vmem),
        compiler_params=pltpu.CompilerParams(vmem_limit_bytes=4 << 20),
    )(table, candidates[0])
    return best[None], scores[None]


def solution(mesh):
    in_specs = (
        P("rep", "shard", None, None),
        P("rep", "shard", None),
        P(("shard", "rep"), None),
        P(),
        P("shard", None),
        P("shard", None, None),
        P("shard"),
    )
    out_specs = (P("rep", "shard", None), P("rep", "shard", None))
    return jax.shard_map(on_device, mesh=mesh, in_specs=in_specs, out_specs=out_specs, check_vma=False)
```

```python
import functools

import jax
import jax.numpy as jnp
from jax import lax
from jax.experimental import pallas as pl
from jax.experimental.pallas import tpu as pltpu
from jax.sharding import PartitionSpec as P


FAR_BELOW = -1e30
LANES = 128
LOW = 256
BOOK_CHUNK = 128
EXACT = lax.Precision.HIGHEST


def exchange(value, axis, mask):
    count = lax.axis_size(axis)
    return lax.ppermute(value, axis, [(i, i ^ mask) for i in range(count)])


def gather_by_xor(block, axis):
    count = lax.axis_size(axis)
    held = block[None]
    reach = 2
    while reach < count:
        step = 2 if reach * 2 == count else 4
        parts = []
        for k in range(step - 1, 0, -1):
            parts.insert(0, exchange(held, axis, reach * k))
        held = jnp.concatenate([held] + parts, axis=0)
        reach *= step
    if count == 1:
        return [held]
    return [held, exchange(held, axis, 1)]


def owner_mask(place, count):
    half = max(1, count // 2)
    return (place % half) * 2 + place // half


def named_rows(total, onehot, high, book_ref, first):
    for j in range(0, book_ref.shape[0] // LOW, 2):
        pair = jnp.concatenate(
            [book_ref[(j + h) * LOW : (j + h + 1) * LOW, :] for h in range(2)], axis=1
        )
        found = jnp.dot(onehot, pair, preferred_element_type=jnp.float32)
        for h in range(2):
            total = jnp.where(high == first + (j + h), found[:, h * LANES : (h + 1) * LANES], total)
    return total


def first_of(k, book_ref):
    return (lax.axis_index("rep") ^ k) * (book_ref.shape[0] // LOW)


def prepare_kernel(
    tokens, ids_hbm, own_hbm, length_hbm, cands_hbm,
    onehot_ref, high_ref, sum_ref, live_ref, mine_ref, owner_ref, column_ref,
    ids_ref, own_ref, length_ref, cands_ref, sems
):
    sources, places = (ids_hbm, own_hbm, length_hbm, cands_hbm), (ids_ref, own_ref, length_ref, cands_ref)
    copies = [pltpu.make_async_copy(*pair, sems.at[i]) for i, pair in enumerate(zip(sources, places))]
    for copy in copies:
        copy.start()
    passages, slots = ids_ref.shape
    shape = mine_ref.shape
    shard = lax.axis_index("shard")
    mask = owner_mask(lax.broadcasted_iota(jnp.int32, shape, 1) // tokens, shape[0])
    mine_ref[...] = ((lax.broadcasted_iota(jnp.int32, shape, 0) ^ shard) == mask).astype(jnp.float32)
    copies[0].wait()
    ids_by_slot = jnp.transpose(ids_ref[...])
    lane = lax.broadcasted_iota(jnp.int32, (slots, LANES), 1)
    first = first_of(0, own_ref)
    for p in range(passages):
        here = pl.ds(p * slots, slots)
        ids = jnp.broadcast_to(ids_by_slot[:, p : p + 1], (slots, LANES))
        low = ids & (LOW - 1)
        onehot_ref[here, :] = jnp.concatenate(
            [(low == lane + k * LANES).astype(jnp.float32) for k in range(LOW // LANES)], axis=1
        ).astype(jnp.bfloat16)
        high_ref[here, :] = ids >> (LOW.bit_length() - 1)
    for copy in copies[1:]:
        copy.wait()
    for p in range(passages):
        live_ref[p : p + 1, :] = jnp.broadcast_to(length_ref[:, p : p + 1], (1, live_ref.shape[1]))
    cands = cands_ref[...]
    owner_ref[...] = (
        lax.broadcasted_iota(jnp.int32, owner_ref.shape, 0) == cands // passages
    ).astype(jnp.float32)
    column_ref[...] = tokens + cands % passages
    for p in range(passages):
        here = pl.ds(p * slots, slots)
        zeros = jnp.zeros((slots, LANES), jnp.float32)
        sum_ref[here, :] = named_rows(zeros, onehot_ref[here, :], high_ref[here, :], own_ref, first)


def fold_kernel(blocks, weight_hbm, codes_hbm, onehot_ref, high_ref, sum_ref, *refs):
    *book_refs, out_ref, residual_ref, weight_ref, codes_ref, sems = refs
    copies = (
        pltpu.make_async_copy(weight_hbm, weight_ref, sems.at[0]),
        pltpu.make_async_copy(codes_hbm, codes_ref, sems.at[1]),
    )
    for copy in copies:
        copy.start()
    passages, slots, _ = codes_ref.shape
    for p in range(passages):
        here = pl.ds(p * slots, slots)
        total = sum_ref[here, :]
        for k, book_ref in zip(blocks, book_refs):
            total = named_rows(total, onehot_ref[here, :], high_ref[here, :], book_ref, first_of(k, book_ref))
        out_ref[here, :] = total
    for copy in copies:
        copy.wait()
    levels = weight_ref.shape[1]
    values = [jnp.broadcast_to(weight_ref[:, k : k + 1], (slots, LANES)) for k in range(levels)]
    for p in range(passages):
        codes = codes_ref[p]
        residual = values[levels - 1]
        for level in range(levels - 2, -1, -1):
            residual = jnp.where(codes == level, values[level], residual)
        residual_ref[pl.ds(p * slots, slots), :] = residual


def score_kernel(
    tokens, parts, live_ref, mine_ref, onehot_ref, high_ref, residual_ref, sum_ref, *refs, last
):
    *book_refs, out_ref, embedded_ref = refs[parts:]
    passages = live_ref.shape[0]
    slots = residual_ref.shape[0] // passages
    queries = jnp.concatenate([ref[...] for ref in refs[:parts]], axis=0)
    width = queries.shape[0]

    def product(rows):
        return lax.dot_general(
            rows, queries, (((1,), (1,)), ((), ())), preferred_element_type=jnp.float32
        )

    best = jnp.full((8, width), FAR_BELOW, jnp.float32)
    for book_ref in book_refs:
        chunk = min(BOOK_CHUNK, book_ref.shape[0])
        for c in range(book_ref.shape[0] // chunk):
            found = product(book_ref[c * chunk : (c + 1) * chunk, :])
            best = jnp.maximum(best, jnp.max(found.reshape(chunk // 8, 8, width), axis=0))
    slot = lax.broadcasted_iota(jnp.int32, (slots, width), 0)
    tops = []
    for p in range(passages):
        here = pl.ds(p * slots, slots)
        total = sum_ref[here, :]
        for k in last:
            total = named_rows(total, onehot_ref[here, :], high_ref[here, :], book_refs[k], first_of(k, book_refs[k]))
        embedded_ref[here, :] = (total + residual_ref[here, :]).astype(jnp.bfloat16)
    for p in range(passages):
        here = pl.ds(p * slots, slots)
        found = jnp.where(slot < live_ref[p : p + 1, :], product(embedded_ref[here, :]), FAR_BELOW)
        tops.append(jnp.max(found, axis=0, keepdims=True))
    best = jnp.max(best, axis=0, keepdims=True)
    room = out_ref.shape[1]
    table = jnp.concatenate(
        [jnp.zeros((tokens, width), jnp.float32)]
        + tops
        + [jnp.zeros((room - tokens - passages, width), jnp.float32)],
        axis=0,
    )
    mine = mine_ref[...]
    sums = lax.dot_general(
        mine, table, (((1,), (1,)), ((), ())), preferred_element_type=jnp.float32, precision=EXACT
    )
    kept = mine * best
    while kept.shape[1] > LANES:
        half = kept.shape[1] // 2
        kept = kept[:, :half] + kept[:, half:]
    shift = LANES // 2
    while shift >= tokens:
        kept = kept + pltpu.roll(kept, shift, 1)
        shift //= 2
    where = lax.broadcasted_iota(jnp.int32, kept.shape, 1)
    rows = jnp.where(where < tokens, kept, sums)
    out_ref[...] = jnp.where(pl.program_id(0) == 0, rows, out_ref[...] + rows)


def finish_kernel(tokens, table_ref, owner_ref, column_ref, best_ref, scores_ref):
    table = table_ref[...]
    best_ref[...] = jnp.max(table, axis=0, keepdims=True)[:, 0:tokens]
    columns = lax.dot_general(
        table, owner_ref[...], (((0,), (0,)), ((), ())), preferred_element_type=jnp.float32, precision=EXACT
    )
    wanted = lax.broadcasted_iota(jnp.int32, columns.shape, 0) == column_ref[...]
    scores_ref[...] = jnp.sum(jnp.where(wanted, columns, 0.0), axis=0, keepdims=True)


def on_device(queries, candidates, codebook, bucket_weights, centroid_ids, residual_codes, passage_lengths):
    tokens, features = queries.shape[2:]
    passages, slots = centroid_ids.shape
    wanted = candidates.shape[2]
    shards, reps = lax.axis_size("shard"), lax.axis_size("rep")
    vmem = pl.BlockSpec(memory_space=pltpu.VMEM)
    rows = passages * slots
    width = min(256, shards * tokens)
    room = LANES

    books = {0: codebook}
    bit = reps // 2
    while bit:
        for k in list(books):
            books[k ^ bit] = exchange(books[k], "rep", bit)
        bit //= 2
    last = (reps - 1,) if reps > 1 else ()
    middle = tuple(k for k in range(1, reps) if k not in last)

    def shaped(*shape, dtype=jnp.float32):
        return jax.ShapeDtypeStruct(shape, dtype)

    def kernel(body, limit=24, **more):
        return pl.pallas_call(
            body,
            compiler_params=pltpu.CompilerParams(vmem_limit_bytes=limit << 20),
            cost_estimate=pl.CostEstimate(flops=1 << 30, bytes_accessed=2 << 20, transcendentals=0),
            **more,
        )

    hbm = pl.BlockSpec(memory_space=pltpu.HBM)

    def in_hbm(value):
        return pltpu.with_memory_space_constraint(value, pltpu.HBM)

    onehot, high, total, live, mine, owner, column = kernel(
        functools.partial(prepare_kernel, tokens),
        out_shape=(
            shaped(rows, LOW, dtype=jnp.bfloat16),
            shaped(rows, LANES, dtype=jnp.int32),
            shaped(rows, features),
            shaped(passages, width, dtype=jnp.int32),
            shaped(shards, shards * tokens),
            shaped(shards, wanted),
            shaped(1, wanted, dtype=jnp.int32),
        ),
        in_specs=[hbm] * 4,
        out_specs=(vmem,) * 7,
        scratch_shapes=[
            pltpu.VMEM(centroid_ids.shape, jnp.int32),
            pltpu.VMEM(codebook.shape, codebook.dtype),
            pltpu.VMEM((1, passages), jnp.int32),
            pltpu.VMEM((1, wanted), jnp.int32),
            pltpu.SemaphoreType.DMA((4,)),
        ],
    )(*map(in_hbm, (centroid_ids, codebook, passage_lengths.reshape(1, passages), candidates[0])))
    groups = [part.reshape(-1, features) for part in gather_by_xor(queries[0, 0], "shard")]
    if shards * tokens > width:
        groups = [jnp.concatenate(groups, axis=0)]
    total, residual = kernel(
        functools.partial(fold_kernel, middle),
        out_shape=(shaped(rows, features), shaped(rows, features)),
        in_specs=[hbm, hbm] + [vmem] * (3 + len(middle)),
        out_specs=(vmem, vmem),
        scratch_shapes=[
            pltpu.VMEM((1, bucket_weights.shape[0]), jnp.float32),
            pltpu.VMEM(residual_codes.shape, jnp.int32),
            pltpu.SemaphoreType.DMA((2,)),
        ],
    )(in_hbm(bucket_weights.reshape(1, -1)), in_hbm(residual_codes), onehot, high, total, *[books[k] for k in middle])

    packed = kernel(
        functools.partial(score_kernel, tokens, len(groups), last=last),
        out_shape=shaped(shards, room),
        grid=(shards * tokens // width,),
        in_specs=[vmem, pl.BlockSpec((shards, width), lambda i: (0, i))]
        + [vmem] * 4
        + [pl.BlockSpec((width // len(groups), features), lambda i: (i, 0))] * len(groups)
        + [vmem] * reps,
        out_specs=vmem,
        scratch_shapes=[pltpu.VMEM((rows, features), jnp.bfloat16)],
    )(live, mine, onehot, high, residual, total, *groups, *[books[k] for k in range(reps)])

    table = lax.all_to_all(packed, "shard", split_axis=0, concat_axis=0, tiled=True)
    best, scores = pl.pallas_call(
        functools.partial(finish_kernel, tokens),
        out_shape=(shaped(1, tokens), shaped(1, wanted)),
        in_specs=[vmem] * 3,
        out_specs=(vmem, vmem),
        compiler_params=pltpu.CompilerParams(vmem_limit_bytes=4 << 20),
    )(table, owner, column)
    return best[None], scores[None]


def solution(mesh):
    in_specs = (
        P("rep", "shard", None, None),
        P("rep", "shard", None),
        P(("shard", "rep"), None),
        P(),
        P("shard", None),
        P("shard", None, None),
        P("shard"),
    )
    out_specs = (P("rep", "shard", None), P("rep", "shard", None))

    return jax.shard_map(on_device, mesh=mesh, in_specs=in_specs, out_specs=out_specs, check_vma=False)
```

```python
import functools

import jax
import jax.numpy as jnp
from jax import lax
from jax.experimental import pallas as pl
from jax.experimental.pallas import tpu as pltpu
from jax.sharding import PartitionSpec as P


FAR_BELOW = -1e30
LANES = 128
LOW = 256
BOOK_CHUNK = 256
PASSAGES = 4
EMBED = (2, 4, 2)
STEPS = lambda high: [high[i : i + 2] for i in range(0, len(high), 2)]


def exchange(value, axis, mask):
    count = lax.axis_size(axis)
    return lax.ppermute(value, axis, [(i, i ^ mask) for i in range(count)])


def steps_of(count):
    high = [1 << i for i in range(1, count.bit_length() - 1)]
    return STEPS(high) + [[1]] if count > 1 else []


def gather_by_xor(block, axis):
    parts = [block[None]]
    for bits in steps_of(lax.axis_size(axis)):
        held = jnp.concatenate(parts, axis=0)
        parts = [held]
        masks = [0]
        for bit in bits:
            masks += [mask | bit for mask in masks]
        sent = {}
        for mask in masks[:0:-1]:
            sent[mask] = exchange(held, axis, mask)
        parts += [sent[mask] for mask in masks[1:]]
    return parts


def owner_mask(place, count):
    bits = sum(steps_of(count), [])
    return sum((((place >> i) & 1) * bit for i, bit in enumerate(bits)), place * 0)


def named_rows(total, onehot, high, book_ref, first):
    for j in range(0, book_ref.shape[0] // LOW, 2):
        pair = jnp.concatenate(
            [book_ref[(j + h) * LOW : (j + h + 1) * LOW, :] for h in range(2)], axis=1
        )
        found = jnp.dot(onehot, pair, preferred_element_type=jnp.float32)
        for h in range(2):
            total = jnp.where(high == first + (j + h), found[:, h * LANES : (h + 1) * LANES], total)
    return total


def first_of(k, book_ref):
    return (lax.axis_index("rep") ^ k) * (book_ref.shape[0] // LOW)


def embed(total_ref, sum_ref, onehot_ref, high_ref, blocks, passages, slots, together):
    many = max(n for n in range(1, together + 1) if passages % n == 0) * slots
    for start in range(0, passages * slots, many):
        here = pl.ds(start, many)
        total = jnp.zeros((many, LANES), jnp.float32) if sum_ref is None else sum_ref[here, :]
        for k, book_ref in blocks:
            total = named_rows(total, onehot_ref[here, :], high_ref[here, :], book_ref, first_of(k, book_ref))
        total_ref[here, :] = total.astype(total_ref.dtype)


def prepare_kernel(
    tokens, near, ids_hbm, own_hbm, weight_hbm, length_hbm, cands_hbm, *refs
):
    near_refs = refs[: len(near)]
    onehot_ref, high_ref, sum_ref, live_ref, mine_ref, owner_ref, column_ref = refs[len(near) : len(near) + 7]
    own_ref, weight_ref, ids_ref, length_ref, cands_ref, sems = refs[len(near) + 7 :]
    copies = [
        pltpu.make_async_copy(source, place, sems.at[i])
        for i, (source, place) in enumerate(
            (
                (ids_hbm, ids_ref),
                (length_hbm, length_ref),
                (cands_hbm, cands_ref),
                (weight_hbm, weight_ref),
                (own_hbm, own_ref),
            )
        )
    ]
    for copy in copies:
        copy.start()
    passages, slots = ids_ref.shape
    shape = mine_ref.shape
    shard = lax.axis_index("shard")
    mask = owner_mask(lax.broadcasted_iota(jnp.int32, shape, 1) // tokens, shape[0])
    mine_ref[...] = ((lax.broadcasted_iota(jnp.int32, shape, 0) ^ shard) == mask).astype(jnp.float32)
    copies[0].wait()
    ids_by_slot = jnp.transpose(ids_ref[...])
    lane = lax.broadcasted_iota(jnp.int32, (slots, LANES), 1)
    for p in range(passages):
        here = pl.ds(p * slots, slots)
        ids = jnp.broadcast_to(ids_by_slot[:, p : p + 1], (slots, LANES))
        low = ids & (LOW - 1)
        onehot_ref[here, :] = jnp.concatenate(
            [(low == lane + k * LANES).astype(jnp.float32) for k in range(LOW // LANES)], axis=1
        ).astype(jnp.bfloat16)
        high_ref[here, :] = ids >> (LOW.bit_length() - 1)
    embed(sum_ref, None, onehot_ref, high_ref, list(zip(near, near_refs)), passages, slots, EMBED[0])
    for copy in copies[1:]:
        copy.wait()
    for p in range(passages):
        live_ref[p : p + 1, :] = jnp.broadcast_to(length_ref[:, p : p + 1], (1, live_ref.shape[1]))
    cands = cands_ref[...]
    wanted = cands.shape[1]
    owner_ref[...] = jnp.zeros(owner_ref.shape, jnp.float32)
    owner_ref[:, 0:wanted] = (
        lax.broadcasted_iota(jnp.int32, (shape[0], wanted), 0) == cands // passages
    ).astype(jnp.float32)
    column_ref[...] = jnp.zeros(column_ref.shape, jnp.int32)
    column_ref[:, 0:wanted] = jnp.broadcast_to(tokens + cands % passages, (shape[0], wanted))


def fold_kernel(blocks, weight_ref, codes_hbm, onehot_ref, high_ref, sum_ref, *refs):
    *book_refs, out_ref, residual_ref, codes_ref, sem = refs
    copy = pltpu.make_async_copy(codes_hbm, codes_ref, sem)
    copy.start()
    passages, slots, _ = codes_ref.shape
    embed(out_ref, sum_ref, onehot_ref, high_ref, list(zip(blocks, book_refs)), passages, slots, EMBED[1])
    levels = weight_ref.shape[1]
    values = [jnp.broadcast_to(weight_ref[:, k : k + 1], (slots, LANES)) for k in range(levels)]
    copy.wait()
    for p in range(passages):
        codes = codes_ref[p]
        residual = values[levels - 1]
        for level in range(levels - 2, -1, -1):
            residual = jnp.where(codes == level, values[level], residual)
        residual_ref[pl.ds(p * slots, slots), :] = residual


def exact_dot(selector, values):
    selector = selector.astype(jnp.bfloat16)
    total = None
    for _ in range(3):
        term = values.astype(jnp.bfloat16)
        values = values - term.astype(jnp.float32)
        found = lax.dot_general(
            selector, term, (((1,), (1,)), ((), ())), preferred_element_type=jnp.float32
        )
        total = found if total is None else total + found
    return total


def scored(tokens, queries, mine, live_ref, embedded_ref, book_refs, room):
    width = queries.shape[0]
    passages = live_ref.shape[0]
    slots = embedded_ref.shape[0] // passages

    nothing = jnp.zeros_like(queries)
    diagonal = jnp.concatenate(
        [jnp.concatenate([queries, nothing], axis=1), jnp.concatenate([nothing, queries], axis=1)], axis=0
    )

    def products(one, two):
        return lax.dot_general(
            jnp.concatenate([one, two], axis=1),
            diagonal,
            (((1,), (1,)), ((), ())),
            preferred_element_type=jnp.float32,
        )

    best = jnp.full((8, 2 * width), FAR_BELOW, jnp.float32)
    for book_ref in book_refs:
        half = book_ref.shape[0] // 2
        chunk = min(BOOK_CHUNK, half)
        for c in range(0, half, chunk):
            found = products(book_ref[c : c + chunk, :], book_ref[half + c : half + c + chunk, :])
            best = jnp.maximum(best, jnp.max(found.reshape(chunk // 8, 8, 2 * width), axis=0))
    best = jnp.max(best, axis=0, keepdims=True)
    best = jnp.maximum(best[:, :width], best[:, width:])
    slot = lax.broadcasted_iota(jnp.int32, (slots, 2 * width), 0)
    half = passages // 2
    tops = [None] * passages
    many = max(n for n in range(1, PASSAGES + 1) if half % n == 0)
    for start in range(0, half, many):
        one, two = (embedded_ref[q * slots : (q + many) * slots, :] for q in (start, start + half))
        together = products(one, two)
        for p in range(start, start + many):
            live = jnp.concatenate([live_ref[q : q + 1, 0:width] for q in (p, p + half)], axis=1)
            found = together[(p - start) * slots : (p - start + 1) * slots, :]
            found = jnp.max(jnp.where(slot < live, found, FAR_BELOW), axis=0, keepdims=True)
            tops[p], tops[p + half] = found[:, :width], found[:, width:]
    table = jnp.concatenate(
        [jnp.zeros((tokens, width), jnp.float32)]
        + tops
        + [jnp.zeros((room - tokens - passages, width), jnp.float32)],
        axis=0,
    )
    sums = exact_dot(mine, table)
    kept = mine * best
    while kept.shape[1] > LANES:
        half = kept.shape[1] // 2
        kept = kept[:, :half] + kept[:, half:]
    shift = kept.shape[1] // 2
    while shift >= tokens:
        kept = kept + pltpu.roll(kept, shift, 1)
        shift //= 2
    where = lax.broadcasted_iota(jnp.int32, kept.shape, 1)
    return jnp.where(where < tokens, kept, sums)


def early_kernel(
    tokens, last, live_ref, mine_ref, onehot_ref, high_ref, residual_ref, sum_ref, query_ref, *refs
):
    *book_refs, out_ref, embedded_ref = refs
    passages = live_ref.shape[0]
    slots = sum_ref.shape[0] // passages

    @pl.when(pl.program_id(0) == 0)
    def _():
        many = max(n for n in range(1, EMBED[2] + 1) if passages % n == 0) * slots
        for start in range(0, passages * slots, many):
            here = pl.ds(start, many)
            total = sum_ref[here, :]
            for k in last:
                book_ref = book_refs[k]
                total = named_rows(total, onehot_ref[here, :], high_ref[here, :], book_ref, first_of(k, book_ref))
            embedded_ref[here, :] = (total + residual_ref[here, :]).astype(jnp.bfloat16)
        out_ref[...] = jnp.zeros(out_ref.shape, jnp.float32)

    room = out_ref.shape[1]
    out_ref[...] += scored(tokens, query_ref[...], mine_ref[...], live_ref, embedded_ref, book_refs, room)


def late_kernel(tokens, live_ref, mine_ref, embedded_ref, early_ref, query_ref, *refs):
    *book_refs, out_ref = refs

    @pl.when(pl.program_id(0) == 0)
    def _():
        out_ref[...] = early_ref[...]

    room = out_ref.shape[1]
    out_ref[...] += scored(tokens, query_ref[...], mine_ref[...], live_ref, embedded_ref, book_refs, room)


def finish_kernel(tokens, table_ref, owner_ref, column_ref, best_ref, scores_ref):
    table = table_ref[...]
    best_ref[...] = jnp.max(table, axis=0, keepdims=True)[:, 0:tokens]
    found = jnp.take_along_axis(table, column_ref[...], axis=1)
    found = jnp.sum(found * owner_ref[...], axis=0, keepdims=True)
    scores_ref[...] = found[:, 0 : scores_ref.shape[1]]


def on_device(queries, candidates, codebook, bucket_weights, centroid_ids, residual_codes, passage_lengths):
    tokens, features = queries.shape[2:]
    passages, slots = centroid_ids.shape
    wanted = candidates.shape[2]
    shards, reps = lax.axis_size("shard"), lax.axis_size("rep")
    vmem = pl.BlockSpec(memory_space=pltpu.VMEM)
    rows = passages * slots
    width = min(LANES, max(shards // 2, 1) * tokens)
    room = LANES

    books = {0: codebook}
    bit = reps // 2
    while bit:
        for k in list(books):
            books[k ^ bit] = exchange(books[k], "rep", bit)
        bit //= 2
    near = tuple(k for k in (1,) if k < reps)
    last = tuple(k for k in (reps - 1,) if k > 1)
    middle = tuple(k for k in range(reps) if k not in near + last)

    def shaped(*shape, dtype=jnp.float32):
        return jax.ShapeDtypeStruct(shape, dtype)

    def kernel(body, limit=24, **more):
        return pl.pallas_call(
            body,
            compiler_params=pltpu.CompilerParams(vmem_limit_bytes=limit << 20),
            cost_estimate=pl.CostEstimate(flops=1 << 30, bytes_accessed=2 << 20, transcendentals=0),
            **more,
        )

    hbm = pl.BlockSpec(memory_space=pltpu.HBM)

    def in_hbm(value):
        return pltpu.with_memory_space_constraint(value, pltpu.HBM)

    onehot, high, total, live, mine, owner, column, own, weights = kernel(
        functools.partial(prepare_kernel, tokens, near),
        out_shape=(
            shaped(rows, LOW, dtype=jnp.bfloat16),
            shaped(rows, LANES, dtype=jnp.int32),
            shaped(rows, features),
            shaped(passages, width, dtype=jnp.int32),
            shaped(shards, shards * tokens),
            shaped(shards, room),
            shaped(shards, room, dtype=jnp.int32),
            shaped(*codebook.shape, dtype=codebook.dtype),
            shaped(1, bucket_weights.shape[0]),
        ),
        in_specs=[hbm] * 5 + [vmem] * len(near),
        out_specs=(vmem,) * 9,
        scratch_shapes=[
            pltpu.VMEM(centroid_ids.shape, jnp.int32),
            pltpu.VMEM((1, passages), jnp.int32),
            pltpu.VMEM((1, wanted), jnp.int32),
            pltpu.SemaphoreType.DMA((5,)),
        ],
    )(
        *map(
            in_hbm,
            (
                centroid_ids,
                codebook,
                bucket_weights.reshape(1, -1),
                passage_lengths.reshape(1, passages),
                candidates[0],
            ),
        ),
        *[books[k] for k in near],
    )
    books[0] = own
    first, *others = [part.reshape(-1, features) for part in gather_by_xor(queries[0, 0], "shard")]
    total, residual = kernel(
        functools.partial(fold_kernel, middle),
        out_shape=(shaped(rows, features), shaped(rows, features)),
        in_specs=[vmem, hbm] + [vmem] * (3 + len(middle)),
        out_specs=(vmem, vmem),
        scratch_shapes=[pltpu.VMEM(residual_codes.shape, jnp.int32), pltpu.SemaphoreType.DMA],
    )(
        weights,
        in_hbm(residual_codes),
        onehot,
        high,
        total,
        *[books[k] for k in middle],
    )

    def queries_spec(start):
        steps = start // width
        return [
            pl.BlockSpec((shards, width), lambda i: (0, i + steps)),
            pl.BlockSpec((width, features), lambda i: (i, 0)),
        ]

    mine_spec, query_spec = queries_spec(0)
    blocks = [books[k] for k in range(reps)]
    packed, embedded = kernel(
        functools.partial(early_kernel, tokens, last),
        out_shape=(shaped(shards, room), shaped(rows, features, dtype=jnp.bfloat16)),
        grid=(first.shape[0] // width,),
        in_specs=[vmem, mine_spec] + [vmem] * 4 + [query_spec] + [vmem] * reps,
        out_specs=(vmem, vmem),
    )(live, mine, onehot, high, residual, total, first, *blocks)
    for other in others:
        mine_spec, query_spec = queries_spec(first.shape[0])
        packed = kernel(
            functools.partial(late_kernel, tokens),
            out_shape=shaped(shards, room),
            grid=(other.shape[0] // width,),
            in_specs=[vmem, mine_spec, vmem, vmem, query_spec] + [vmem] * reps,
            out_specs=vmem,
        )(live, mine, embedded, packed, other, *blocks)

    table = lax.all_to_all(packed, "shard", split_axis=0, concat_axis=0, tiled=True)
    best, scores = pl.pallas_call(
        functools.partial(finish_kernel, tokens),
        out_shape=(shaped(1, tokens), shaped(1, wanted)),
        in_specs=[vmem] * 3,
        out_specs=(vmem, vmem),
        compiler_params=pltpu.CompilerParams(vmem_limit_bytes=4 << 20),
    )(table, owner, column)
    return best[None], scores[None]


def solution(mesh):
    in_specs = (
        P("rep", "shard", None, None),
        P("rep", "shard", None),
        P(("shard", "rep"), None),
        P(),
        P("shard", None),
        P("shard", None, None),
        P("shard"),
    )
    out_specs = (P("rep", "shard", None), P("rep", "shard", None))

    return jax.shard_map(on_device, mesh=mesh, in_specs=in_specs, out_specs=out_specs, check_vma=False)
```

```python
import functools

import jax
import jax.numpy as jnp
from jax import lax
from jax.experimental import pallas as pl
from jax.experimental.pallas import tpu as pltpu
from jax.sharding import PartitionSpec as P


FAR_BELOW = -1e30
LANES = 128
LOW = 256
BOOK_CHUNK = 256
PASSAGES = 4
EMBED = (2, 4, 2)
STEPS = lambda high: [high[i : i + 2] for i in range(0, len(high), 2)]


def exchange(value, axis, mask):
    count = lax.axis_size(axis)
    return lax.ppermute(value, axis, [(i, i ^ mask) for i in range(count)])


def steps_of(count):
    high = [1 << i for i in range(1, count.bit_length() - 1)]
    return STEPS(high) + [[1]] if count > 1 else []


def gather_by_xor(block, axis):
    parts = [block[None]]
    for bits in steps_of(lax.axis_size(axis)):
        held = jnp.concatenate(parts, axis=0)
        parts = [held]
        masks = [0]
        for bit in bits:
            masks += [mask | bit for mask in masks]
        sent = {}
        for mask in masks[:0:-1]:
            sent[mask] = exchange(held, axis, mask)
        parts += [sent[mask] for mask in masks[1:]]
    return parts


def owner_mask(place, count):
    bits = sum(steps_of(count), [])
    return sum((((place >> i) & 1) * bit for i, bit in enumerate(bits)), place * 0)


def named_rows(total, onehot, high, book_ref, first):
    for j in range(0, book_ref.shape[0] // LOW, 2):
        pair = jnp.concatenate(
            [book_ref[(j + h) * LOW : (j + h + 1) * LOW, :] for h in range(2)], axis=1
        )
        found = jnp.dot(onehot, pair, preferred_element_type=jnp.float32)
        for h in range(2):
            total = jnp.where(high == first + (j + h), found[:, h * LANES : (h + 1) * LANES], total)
    return total


def first_of(k, book_ref):
    return (lax.axis_index("rep") ^ k) * (book_ref.shape[0] // LOW)


def embed(total_ref, sum_ref, onehot_ref, high_ref, blocks, passages, slots, together):
    many = max(n for n in range(1, together + 1) if passages % n == 0) * slots
    for start in range(0, passages * slots, many):
        here = pl.ds(start, many)
        total = jnp.zeros((many, LANES), jnp.float32) if sum_ref is None else sum_ref[here, :]
        for k, book_ref in blocks:
            total = named_rows(total, onehot_ref[here, :], high_ref[here, :], book_ref, first_of(k, book_ref))
        total_ref[here, :] = total.astype(total_ref.dtype)


def prepare_kernel(
    tokens, near, ids_hbm, own_hbm, weight_hbm, length_hbm, cands_hbm, *refs
):
    near_refs = refs[: len(near)]
    onehot_ref, high_ref, sum_ref, live_ref, mine_ref, owner_ref, column_ref = refs[len(near) : len(near) + 7]
    own_ref, weight_ref, ids_ref, length_ref, cands_ref, sems = refs[len(near) + 7 :]
    copies = [
        pltpu.make_async_copy(source, place, sems.at[i])
        for i, (source, place) in enumerate(
            (
                (ids_hbm, ids_ref),
                (length_hbm, length_ref),
                (cands_hbm, cands_ref),
                (weight_hbm, weight_ref),
                (own_hbm, own_ref),
            )
        )
    ]
    for copy in copies:
        copy.start()
    passages, slots = ids_ref.shape
    shape = mine_ref.shape
    shard = lax.axis_index("shard")
    mask = owner_mask(lax.broadcasted_iota(jnp.int32, shape, 1) // tokens, shape[0])
    mine_ref[...] = ((lax.broadcasted_iota(jnp.int32, shape, 0) ^ shard) == mask).astype(jnp.float32)
    copies[0].wait()
    ids_by_slot = jnp.transpose(ids_ref[...])
    lane = lax.broadcasted_iota(jnp.int32, (slots, LANES), 1)
    for p in range(passages):
        here = pl.ds(p * slots, slots)
        ids = jnp.broadcast_to(ids_by_slot[:, p : p + 1], (slots, LANES))
        low = ids & (LOW - 1)
        onehot_ref[here, :] = jnp.concatenate(
            [(low == lane + k * LANES).astype(jnp.float32) for k in range(LOW // LANES)], axis=1
        ).astype(jnp.bfloat16)
        high_ref[here, :] = ids >> (LOW.bit_length() - 1)
    embed(sum_ref, None, onehot_ref, high_ref, list(zip(near, near_refs)), passages, slots, EMBED[0])
    for copy in copies[1:]:
        copy.wait()
    for p in range(passages):
        live_ref[p : p + 1, :] = jnp.broadcast_to(length_ref[:, p : p + 1], (1, live_ref.shape[1]))
    cands = cands_ref[...]
    wanted = cands.shape[1]
    owner_ref[...] = jnp.zeros(owner_ref.shape, jnp.float32)
    owner_ref[:, 0:wanted] = (
        lax.broadcasted_iota(jnp.int32, (shape[0], wanted), 0) == cands // passages
    ).astype(jnp.float32)
    column_ref[...] = jnp.zeros(column_ref.shape, jnp.int32)
    column_ref[:, 0:wanted] = jnp.broadcast_to(tokens + cands % passages, (shape[0], wanted))


def fold_kernel(blocks, weight_ref, codes_hbm, onehot_ref, high_ref, sum_ref, *refs):
    *book_refs, out_ref, residual_ref, codes_ref, sem = refs
    copy = pltpu.make_async_copy(codes_hbm, codes_ref, sem)
    copy.start()
    passages, slots, _ = codes_ref.shape
    embed(out_ref, sum_ref, onehot_ref, high_ref, list(zip(blocks, book_refs)), passages, slots, EMBED[1])
    levels = weight_ref.shape[1]
    values = [jnp.broadcast_to(weight_ref[:, k : k + 1], (slots, LANES)) for k in range(levels)]
    copy.wait()
    for p in range(passages):
        codes = codes_ref[p]
        residual = values[levels - 1]
        for level in range(levels - 2, -1, -1):
            residual = jnp.where(codes == level, values[level], residual)
        residual_ref[pl.ds(p * slots, slots), :] = residual


def exact_dot(selector, values):
    terms = []
    for _ in range(3):
        terms.append(values.astype(jnp.bfloat16))
        values = values - terms[-1].astype(jnp.float32)
    return lax.dot_general(
        jnp.concatenate([selector.astype(jnp.bfloat16)] * 3, axis=1),
        jnp.concatenate(terms, axis=1),
        (((1,), (1,)), ((), ())),
        preferred_element_type=jnp.float32,
    )


def scored(tokens, queries, mine, live_ref, embedded_ref, book_refs, room):
    width = queries.shape[0]
    passages = live_ref.shape[0]
    slots = embedded_ref.shape[0] // passages

    nothing = jnp.zeros_like(queries)
    diagonal = jnp.concatenate(
        [jnp.concatenate([queries, nothing], axis=1), jnp.concatenate([nothing, queries], axis=1)], axis=0
    )

    def products(one, two):
        return lax.dot_general(
            jnp.concatenate([one, two], axis=1),
            diagonal,
            (((1,), (1,)), ((), ())),
            preferred_element_type=jnp.float32,
        )

    best = jnp.full((8, 2 * width), FAR_BELOW, jnp.float32)
    for book_ref in book_refs:
        half = book_ref.shape[0] // 2
        chunk = min(BOOK_CHUNK, half)
        for c in range(0, half, chunk):
            found = products(book_ref[c : c + chunk, :], book_ref[half + c : half + c + chunk, :])
            best = jnp.maximum(best, jnp.max(found.reshape(chunk // 8, 8, 2 * width), axis=0))
    best = jnp.max(best, axis=0, keepdims=True)
    best = jnp.maximum(best[:, :width], best[:, width:])
    slot = lax.broadcasted_iota(jnp.int32, (slots, 2 * width), 0)
    half = passages // 2
    tops = [None] * passages
    many = max(n for n in range(1, PASSAGES + 1) if half % n == 0)
    for start in range(0, half, many):
        one, two = (embedded_ref[q * slots : (q + many) * slots, :] for q in (start, start + half))
        together = products(one, two)
        for p in range(start, start + many):
            live = jnp.concatenate([live_ref[q : q + 1, 0:width] for q in (p, p + half)], axis=1)
            found = together[(p - start) * slots : (p - start + 1) * slots, :]
            found = jnp.max(jnp.where(slot < live, found, FAR_BELOW), axis=0, keepdims=True)
            tops[p], tops[p + half] = found[:, :width], found[:, width:]
    table = jnp.concatenate(
        [jnp.zeros((tokens, width), jnp.float32)]
        + tops
        + [jnp.zeros((room - tokens - passages, width), jnp.float32)],
        axis=0,
    )
    sums = exact_dot(mine, table)
    kept = mine * best
    while kept.shape[1] > LANES:
        half = kept.shape[1] // 2
        kept = kept[:, :half] + kept[:, half:]
    shift = kept.shape[1] // 2
    while shift >= tokens:
        kept = kept + pltpu.roll(kept, shift, 1)
        shift //= 2
    where = lax.broadcasted_iota(jnp.int32, kept.shape, 1)
    return jnp.where(where < tokens, kept, sums)


def early_kernel(
    tokens, last, live_ref, mine_ref, onehot_ref, high_ref, residual_ref, sum_ref, query_ref, *refs
):
    *book_refs, out_ref, embedded_ref = refs
    passages = live_ref.shape[0]
    slots = sum_ref.shape[0] // passages

    @pl.when(pl.program_id(0) == 0)
    def _():
        many = max(n for n in range(1, EMBED[2] + 1) if passages % n == 0) * slots
        for start in range(0, passages * slots, many):
            here = pl.ds(start, many)
            total = sum_ref[here, :]
            for k in last:
                book_ref = book_refs[k]
                total = named_rows(total, onehot_ref[here, :], high_ref[here, :], book_ref, first_of(k, book_ref))
            embedded_ref[here, :] = (total + residual_ref[here, :]).astype(jnp.bfloat16)
        out_ref[...] = jnp.zeros(out_ref.shape, jnp.float32)

    room = out_ref.shape[1]
    out_ref[...] += scored(tokens, query_ref[...], mine_ref[...], live_ref, embedded_ref, book_refs, room)


def late_kernel(tokens, live_ref, mine_ref, embedded_ref, early_ref, query_ref, *refs):
    *book_refs, out_ref = refs

    @pl.when(pl.program_id(0) == 0)
    def _():
        out_ref[...] = early_ref[...]

    room = out_ref.shape[1]
    out_ref[...] += scored(tokens, query_ref[...], mine_ref[...], live_ref, embedded_ref, book_refs, room)


def finish_kernel(tokens, table_ref, owner_ref, column_ref, best_ref, scores_ref):
    table = table_ref[...]
    best_ref[...] = jnp.max(table, axis=0, keepdims=True)[:, 0:tokens]
    found = jnp.take_along_axis(table, column_ref[...], axis=1)
    found = jnp.sum(found * owner_ref[...], axis=0, keepdims=True)
    scores_ref[...] = found[:, 0 : scores_ref.shape[1]]


def on_device(queries, candidates, codebook, bucket_weights, centroid_ids, residual_codes, passage_lengths):
    tokens, features = queries.shape[2:]
    passages, slots = centroid_ids.shape
    wanted = candidates.shape[2]
    shards, reps = lax.axis_size("shard"), lax.axis_size("rep")
    vmem = pl.BlockSpec(memory_space=pltpu.VMEM)
    rows = passages * slots
    width = min(LANES, max(shards // 2, 1) * tokens)
    room = LANES

    books = {0: codebook}
    bit = reps // 2
    while bit:
        for k in list(books):
            books[k ^ bit] = exchange(books[k], "rep", bit)
        bit //= 2
    near = tuple(k for k in (1,) if k < reps)
    last = tuple(k for k in (reps - 1,) if k > 1)
    middle = tuple(k for k in range(reps) if k not in near + last)

    def shaped(*shape, dtype=jnp.float32):
        return jax.ShapeDtypeStruct(shape, dtype)

    def kernel(body, limit=24, **more):
        return pl.pallas_call(
            body,
            compiler_params=pltpu.CompilerParams(vmem_limit_bytes=limit << 20),
            cost_estimate=pl.CostEstimate(flops=1 << 30, bytes_accessed=2 << 20, transcendentals=0),
            **more,
        )

    hbm = pl.BlockSpec(memory_space=pltpu.HBM)

    def in_hbm(value):
        return pltpu.with_memory_space_constraint(value, pltpu.HBM)

    onehot, high, total, live, mine, owner, column, own, weights = kernel(
        functools.partial(prepare_kernel, tokens, near),
        out_shape=(
            shaped(rows, LOW, dtype=jnp.bfloat16),
            shaped(rows, LANES, dtype=jnp.int32),
            shaped(rows, features),
            shaped(passages, width, dtype=jnp.int32),
            shaped(shards, shards * tokens),
            shaped(shards, room),
            shaped(shards, room, dtype=jnp.int32),
            shaped(*codebook.shape, dtype=codebook.dtype),
            shaped(1, bucket_weights.shape[0]),
        ),
        in_specs=[hbm] * 5 + [vmem] * len(near),
        out_specs=(vmem,) * 9,
        scratch_shapes=[
            pltpu.VMEM(centroid_ids.shape, jnp.int32),
            pltpu.VMEM((1, passages), jnp.int32),
            pltpu.VMEM((1, wanted), jnp.int32),
            pltpu.SemaphoreType.DMA((5,)),
        ],
    )(
        *map(
            in_hbm,
            (
                centroid_ids,
                codebook,
                bucket_weights.reshape(1, -1),
                passage_lengths.reshape(1, passages),
                candidates[0],
            ),
        ),
        *[books[k] for k in near],
    )
    books[0] = own
    first, *others = [part.reshape(-1, features) for part in gather_by_xor(queries[0, 0], "shard")]
    total, residual = kernel(
        functools.partial(fold_kernel, middle),
        out_shape=(shaped(rows, features), shaped(rows, features)),
        in_specs=[vmem, hbm] + [vmem] * (3 + len(middle)),
        out_specs=(vmem, vmem),
        scratch_shapes=[pltpu.VMEM(residual_codes.shape, jnp.int32), pltpu.SemaphoreType.DMA],
    )(
        weights,
        in_hbm(residual_codes),
        onehot,
        high,
        total,
        *[books[k] for k in middle],
    )

    def queries_spec(start):
        steps = start // width
        return [
            pl.BlockSpec((shards, width), lambda i: (0, i + steps)),
            pl.BlockSpec((width, features), lambda i: (i, 0)),
        ]

    mine_spec, query_spec = queries_spec(0)
    blocks = [books[k] for k in range(reps)]
    packed, embedded = kernel(
        functools.partial(early_kernel, tokens, last),
        out_shape=(shaped(shards, room), shaped(rows, features, dtype=jnp.bfloat16)),
        grid=(first.shape[0] // width,),
        in_specs=[vmem, mine_spec] + [vmem] * 4 + [query_spec] + [vmem] * reps,
        out_specs=(vmem, vmem),
    )(live, mine, onehot, high, residual, total, first, *blocks)
    for other in others:
        mine_spec, query_spec = queries_spec(first.shape[0])
        packed = kernel(
            functools.partial(late_kernel, tokens),
            out_shape=shaped(shards, room),
            grid=(other.shape[0] // width,),
            in_specs=[vmem, mine_spec, vmem, vmem, query_spec] + [vmem] * reps,
            out_specs=vmem,
        )(live, mine, embedded, packed, other, *blocks)

    table = lax.all_to_all(packed, "shard", split_axis=0, concat_axis=0, tiled=True)
    best, scores = pl.pallas_call(
        functools.partial(finish_kernel, tokens),
        out_shape=(shaped(1, tokens), shaped(1, wanted)),
        in_specs=[vmem] * 3,
        out_specs=(vmem, vmem),
        compiler_params=pltpu.CompilerParams(vmem_limit_bytes=4 << 20),
    )(table, owner, column)
    return best[None], scores[None]


def solution(mesh):
    in_specs = (
        P("rep", "shard", None, None),
        P("rep", "shard", None),
        P(("shard", "rep"), None),
        P(),
        P("shard", None),
        P("shard", None, None),
        P("shard"),
    )
    out_specs = (P("rep", "shard", None), P("rep", "shard", None))

    return jax.shard_map(on_device, mesh=mesh, in_specs=in_specs, out_specs=out_specs, check_vma=False)
```
